32 devices in a mesh: dp: 4 (over z), row: 2 (over x), col: 4 (over y, core).
Axes of the slice: x: 2, y: 2, z: 4, core: 2. Of those that a mesh axis runs over, the one named last changes fastest.
Arguments:
- hidden_in: bfloat16 [4, 512, 2048], P('dp', 'row'), may hold values from -6 to 6
- out_grad: bfloat16 [4, 512, 2048], P('dp', 'row'), may hold values from -6 to 6
- seg_ids: int32 [4, 512], P('dp'), may hold values from 0 to 5, as said below
- seg_starts: int32 [4, 512], P('dp', 'row'), may hold values from 0 to 1, as said below
- input_gain: float32 [2048], replicated, may hold values from 0.5 to 1.5
- middle_gain: float32 [2048], replicated, may hold values from 0.5 to 1.5
- mixer_gain: float32 [3072], P('col'), may hold values from 0.5 to 1.5
- conv_input_weight: float32 [4, 3072], P(None, 'col'), may hold values from -0.5 to 0.5
- conv_input_bias: float32 [3072], P('col'), may hold values from -0.5 to 0.5
- conv_state_weight: float32 [4, 512], P(None, 'col'), may hold values from -0.5 to 0.5
- conv_state_bias: float32 [512], P('col'), may hold values from -0.5 to 0.5
- log_rates: float32 [48], P('col'), may hold values from -1 to 1.5
- step_bias: float32 [48], P('col'), may hold values from -7 to -3
- skip_gain: float32 [48], P('col'), may hold values from 0.5 to 1.5
- mixer_gate: bfloat16 [2048, 3072], P('row', 'col'), may hold values from -0.125 to 0.125
- mixer_input: bfloat16 [2048, 3072], P('row', 'col'), may hold values from -0.125 to 0.125
- step_weight: bfloat16 [2048, 48], P('row', 'col'), may hold values from -0.0625 to 0.0625
- state_weight: bfloat16 [2048, 512], P('row', 'col'), may hold values from -0.125 to 0.125
- query_weight: bfloat16 [2048, 1024], P('row', 'col'), may hold values from -0.125 to 0.125
- key_value_weight: bfloat16 [2048, 512], P('row', 'col'), may hold values from -0.125 to 0.125
- mixer_output: bfloat16 [3072, 2048], P('col', 'row'), may hold values from -0.109375 to 0.109375
- attention_out: bfloat16 [1024, 2048], P('col', 'row'), may hold values from -0.75 to 0.75
- gate_weight: bfloat16 [2048, 4096], P('row', 'col'), may hold values from -0.125 to 0.125
- up_weight: bfloat16 [2048, 4096], P('row', 'col'), may hold values from -0.125 to 0.125
- down_weight: bfloat16 [4096, 2048], P('col', 'row'), may hold values from -0.09375 to 0.09375
Outputs:
- hidden_out: bfloat16 [4, 512, 2048], P('dp', 'row')
- grad_in: float32 [4, 512, 2048], P('dp', 'row')
- grad_input_gain: float32 [2048], replicated
- grad_middle_gain: float32 [2048], replicated
- grad_mixer_gain: float32 [3072], P('col')
- grad_conv_input_weight: float32 [4, 3072], P(None, 'col')
- grad_conv_input_bias: float32 [3072], P('col')
- grad_conv_state_weight: float32 [4, 512], P(None, 'col')
- grad_conv_state_bias: float32 [512], P('col')
- grad_log_rates: float32 [48], P('col')
- grad_step_bias: float32 [48], P('col')
- grad_skip_gain: float32 [48], P('col')
- grad_mixer_gate: float32 [2048, 3072], P(('dp', 'row'), 'col')
- grad_mixer_input: float32 [2048, 3072], P(('dp', 'row'), 'col')
- grad_step_weight: float32 [2048, 48], P(('dp', 'row'), 'col')
- grad_state_weight: float32 [2048, 512], P(('dp', 'row'), 'col')
- grad_query_weight: float32 [2048, 1024], P(('dp', 'row'), 'col')
- grad_keyval_weight: float32 [2048, 512], P(('dp', 'row'), 'col')
- grad_mixer_output: float32 [3072, 2048], P('col', ('dp', 'row'))
- grad_attention_out: float32 [1024, 2048], P('col', ('dp', 'row'))
- grad_gate_weight: float32 [2048, 4096], P(('dp', 'row'), 'col')
- grad_up_weight: float32 [2048, 4096], P(('dp', 'row'), 'col')
- grad_down_weight: float32 [4096, 2048], P('col', ('dp', 'row'))
The draws below stay inside these ranges and needn't reach their ends.
Inputs may be any that keep to these rules, and one draw needn't show every extreme that they name: `seg_ids`: along each sequence the ids begin at 0 and rise by 0 or 1 from one token to the next; each sequence holds exactly 6 documents, so its last token has the id 6 - 1. `seg_starts`: 1 at each sequence's first token and wherever seg_ids changes, 0 elsewhere.
All inputs are finite; a program needn't handle non-finite values.
Results may differ from the reference program's by a relative error of at most 0.019.
Values may be sent and summed in bfloat16 or wider, within the bound.
No kernel may reach another device: no remote copies, remote signals or barrier semaphores. Data moves between devices by JAX's collectives and lax.ppermute only.
A program may use at most 104 MiB of HBM per device.

```python
import math
import jax
import jax.numpy as jnp
from jax import lax

MODEL_WIDTH = 2048
HM = 48
HP = 64
NS = 256
CONV = 4
QUERY_HEADS_TOTAL = 8
KEYVALUE_HEADS = 2
HEAD_SIZE = 128
FF = 4096
DOCS = 6
DI = 3072
LEN = 512
SEQS = 4


def segment_layout(key):
    sequence_keys = jax.random.split(jax.random.fold_in(key, 7), SEQS)
    places = jnp.arange(1, LEN, dtype=jnp.int32)
    window = LEN // 8

    def cut_points(one_key):
        order_key, start_key = jax.random.split(one_key)
        shuffled = jax.random.permutation(order_key, LEN - 1).astype(jnp.int32)
        window_start = jax.random.randint(start_key, (), 1, LEN - window + 1, dtype=jnp.int32)
        inside = (places >= window_start) & (places < window_start + window)
        inner_scores = jnp.where(inside, shuffled, -1)
        outer_scores = jnp.where(inside, -1, shuffled)
        inner_index = jax.lax.top_k(inner_scores, 2)[1]
        outer_index = jax.lax.top_k(outer_scores, DOCS - 3)[1]
        return jnp.concatenate([places[inner_index], places[outer_index]]).astype(jnp.int32)
    cuts = jax.vmap(cut_points)(sequence_keys)
    positions = jnp.arange(LEN, dtype=jnp.int32)
    passed = (cuts[:, None, :] <= positions[None, :, None]).astype(jnp.int32)
    return jnp.sum(passed, axis=2).astype(jnp.int32)


def draw_seg_ids(key, part):
    return segment_layout(key)


def draw_seg_starts(key, part):
    ids_drawn = segment_layout(key)
    prior = jnp.concatenate([jnp.full((SEQS, 1), -1, jnp.int32), ids_drawn[:, :-1]], axis=1)
    return (ids_drawn != prior).astype(jnp.int32)


def steps_of(own_key, dims, cuts, low, top_value):
    level = 1.0
    for dim, blocks in cuts:
        heights = jax.random.uniform(jax.random.fold_in(jax.random.fold_in(own_key, 6), dim), (blocks,), jnp.float32, low / len(cuts), top_value / len(cuts))
        level = level * jnp.repeat(jnp.exp(heights), dims[dim] // blocks).reshape((-1,) + (1,) * (len(dims) - 1 - dim))
    return level


def noise(key, extent, deviation, limit, cuts=(), held_as=jnp.bfloat16):
    drawn = deviation * jax.random.normal(key, extent, jnp.float32)
    if cuts:
        drawn = drawn * steps_of(key, extent, cuts, -0.22, 0.18)
    return jnp.clip(drawn, -limit, limit).astype(held_as)


def setup_inputs(seed: int = 0) -> dict:
    key_list = jax.random.split(jax.random.key(seed), 26)
    return {
        "hidden_in": noise(key_list[0], (SEQS, LEN, MODEL_WIDTH), 1.0, 6.0, ((0, 4), (1, 2))),
        "out_grad": noise(key_list[1], (SEQS, LEN, MODEL_WIDTH), 1.0, 6.0, ((0, 4), (1, 2))),
        "seg_ids": draw_seg_ids(jax.random.fold_in(key_list[25], 71), 0),
        "seg_starts": draw_seg_starts(jax.random.fold_in(key_list[25], 71), 0),
        "input_gain": jnp.clip(1.0 + 0.1 * jax.random.normal(key_list[4], (MODEL_WIDTH,), jnp.float32), 0.5, 1.5),
        "middle_gain": jnp.clip(1.0 + 0.1 * jax.random.normal(key_list[5], (MODEL_WIDTH,), jnp.float32), 0.5, 1.5),
        "mixer_gain": jnp.clip(1.0 + 0.1 * jax.random.normal(key_list[6], (DI,), jnp.float32), 0.5, 1.5),
        "conv_input_weight": jnp.clip(jax.random.uniform(key_list[7], (CONV, DI), jnp.float32, -0.5, 0.5) * steps_of(key_list[7], (CONV, DI), ((1, 4),), -0.4, 0.0), -0.5, 0.5),
        "conv_input_bias": jnp.clip(jax.random.uniform(key_list[8], (DI,), jnp.float32, -0.5, 0.5) * steps_of(key_list[8], (DI,), ((0, 4),), -0.4, 0.0), -0.5, 0.5),
        "conv_state_weight": jnp.clip(jax.random.uniform(key_list[9], (CONV, 2 * NS), jnp.float32, -0.5, 0.5) * steps_of(key_list[9], (CONV, 2 * NS), ((1, 4),), -0.4, 0.0), -0.5, 0.5),
        "conv_state_bias": jnp.clip(jax.random.uniform(key_list[10], (2 * NS,), jnp.float32, -0.5, 0.5) * steps_of(key_list[10], (2 * NS,), ((0, 4),), -0.4, 0.0), -0.5, 0.5),
        "log_rates": jnp.clip(-1.0 + 2.5 * jax.random.uniform(key_list[11], (HM,), jnp.float32) ** steps_of(key_list[11], (HM,), ((0, 4),), -0.2, 0.2), -1.0, 1.5),
        "step_bias": jnp.clip(-7.0 + 4.0 * jax.random.uniform(key_list[12], (HM,), jnp.float32) ** steps_of(key_list[12], (HM,), ((0, 4),), -0.2, 0.2), -7.0, -3.0),
        "skip_gain": jnp.clip(0.5 + 1.0 * jax.random.uniform(key_list[13], (HM,), jnp.float32) ** steps_of(key_list[13], (HM,), ((0, 4),), -0.2, 0.2), 0.5, 1.5),
        "mixer_gate": noise(key_list[14], (MODEL_WIDTH, DI), MODEL_WIDTH ** -0.5, 0.125, ((0, 2), (1, 4))),
        "mixer_input": noise(key_list[15], (MODEL_WIDTH, DI), MODEL_WIDTH ** -0.5, 0.125, ((0, 2), (1, 4))),
        "step_weight": noise(key_list[16], (MODEL_WIDTH, HM), (4 * MODEL_WIDTH) ** -0.5, 0.0625, ((0, 2), (1, 4))),
        "state_weight": noise(key_list[17], (MODEL_WIDTH, 2 * NS), MODEL_WIDTH ** -0.5, 0.125, ((0, 2), (1, 4))),
        "query_weight": noise(key_list[18], (MODEL_WIDTH, QUERY_HEADS_TOTAL * HEAD_SIZE), MODEL_WIDTH ** -0.5, 0.125, ((0, 2), (1, 4))),
        "key_value_weight": noise(key_list[19], (MODEL_WIDTH, 2 * KEYVALUE_HEADS * HEAD_SIZE), MODEL_WIDTH ** -0.5, 0.125, ((0, 2), (1, 4))),
        "mixer_output": noise(key_list[20], (DI, MODEL_WIDTH), DI ** -0.5, 0.109375, ((0, 4), (1, 2))),
        "attention_out": noise(key_list[21], (QUERY_HEADS_TOTAL * HEAD_SIZE, MODEL_WIDTH), (QUERY_HEADS_TOTAL * HEAD_SIZE // 16) ** -0.5, 0.75, ((0, 4), (1, 2))),
        "gate_weight": noise(key_list[22], (MODEL_WIDTH, FF), MODEL_WIDTH ** -0.5, 0.125, ((0, 2), (1, 4))),
        "up_weight": noise(key_list[23], (MODEL_WIDTH, FF), MODEL_WIDTH ** -0.5, 0.125, ((0, 2), (1, 4))),
        "down_weight": noise(key_list[24], (FF, MODEL_WIDTH), FF ** -0.5, 0.09375, ((0, 4), (1, 2))),
    }


EPSILON = 1e-05
HIGHEST = lax.Precision.HIGHEST

@jax.custom_vjp
def low(v):
    return lax.optimization_barrier(v.astype(jnp.bfloat16)).astype(jnp.float32)

@jax.custom_vjp
def low_back(v):
    return v

def low_keep(v):
    return (low(v), None)

def low_pass(kept, grad):
    return (grad,)

def back_keep(v):
    return (v, None)

def back_low(kept, grad):
    return (low(grad),)
low.defvjp(low_keep, low_pass)
low_back.defvjp(back_keep, back_low)

def matmul_high(left, right):
    return jnp.dot(left, right, precision=HIGHEST, preferred_element_type=jnp.float32)

def rms_norm(values, gain):
    return values * lax.rsqrt(lax.optimization_barrier(jnp.mean(values * values, axis=-1, keepdims=True)) + EPSILON) * gain

def conv_mix(extended, conv_weight, conv_bias, seg_row, positions):
    tokens = positions.shape[0]
    sequence_length = seg_row.shape[0]
    summed = jnp.zeros((tokens, extended.shape[1]), jnp.float32) + conv_bias
    own_seg = seg_row[positions]
    for offset in range(CONV):
        source = positions - offset
        usable = (source >= 0) & (seg_row[jnp.clip(source, 0, sequence_length - 1)] == own_seg)
        shifted = extended[CONV - 1 - offset:CONV - 1 - offset + tokens]
        summed = summed + jnp.where(usable[:, None], shifted, 0.0) * conv_weight[CONV - 1 - offset]
    return jax.nn.silu(summed)

def ssd_block(carried, block_parts):
    input_part, bterm_part, cterm_part, step_part, decay_part, start_part = block_parts
    width = start_part.shape[0]
    cumulative = jnp.cumsum(decay_part, axis=0)
    run_ids = jnp.cumsum(start_part)
    ordinal = jnp.arange(width)
    joined = (ordinal[:, None] >= ordinal[None, :]) & (run_ids[:, None] == run_ids[None, :])
    spread = cumulative[:, None, :] - cumulative[None, :, :]
    factor = jnp.exp(jnp.where(joined[:, :, None], spread, 0.0)) * joined[:, :, None].astype(jnp.float32)
    inner_cb = jnp.einsum('tn,sn->ts', cterm_part, bterm_part, precision=HIGHEST)
    mixing = inner_cb[:, :, None] * factor * step_part[None, :, :]
    output = jnp.einsum('tsh,shp->thp', mixing, input_part, precision=HIGHEST)
    entry_keep = jnp.exp(cumulative) * (run_ids == 0)[:, None].astype(jnp.float32)
    output = output + entry_keep[:, :, None] * jnp.einsum('tn,hpn->thp', cterm_part, carried, precision=HIGHEST)
    to_end = jnp.exp(cumulative[-1][None, :] - cumulative) * (run_ids == run_ids[-1])[:, None].astype(jnp.float32)
    carry_on = jnp.exp(cumulative[-1]) * (run_ids[-1] == 0).astype(jnp.float32)
    weighted = (to_end * step_part)[:, :, None] * input_part
    update = jnp.einsum('shp,sn->hpn', weighted, bterm_part, precision=HIGHEST)
    return (carry_on[:, None, None] * carried + update, output)

def ssd_scan(head_inputs, input_matrix, output_matrix, step_size, decay_log, starts):
    tokens, head_count, head_width = head_inputs.shape
    block_length = math.gcd(tokens, 128)
    block_count = tokens // block_length
    block_parts = (head_inputs.reshape(block_count, block_length, head_count, head_width), input_matrix.reshape(block_count, block_length, -1), output_matrix.reshape(block_count, block_length, -1), step_size.reshape(block_count, block_length, head_count), decay_log.reshape(block_count, block_length, head_count), starts.reshape(block_count, block_length))
    initial = jnp.zeros((head_count, head_width, input_matrix.shape[1]), jnp.float32)
    last_state, outputs = lax.scan(jax.checkpoint(ssd_block), initial, block_parts)
    return outputs.reshape(tokens, head_count, head_width)

def attend(query_rows, key_heads, value_heads, seg_row):
    sequence_length = query_rows.shape[0]
    group_width = QUERY_HEADS_TOTAL // KEYVALUE_HEADS
    block_length = math.gcd(sequence_length, 512)
    places = jnp.arange(sequence_length, dtype=jnp.int32)

    def one_block(number):
        anchor_position = (number * block_length).astype(jnp.int32)
        row_ids = anchor_position + jnp.arange(block_length, dtype=jnp.int32)
        block_of_queries = lax.dynamic_slice_in_dim(query_rows, anchor_position, block_length, 0).reshape(block_length, KEYVALUE_HEADS, group_width, HEAD_SIZE)
        raw_scores = jnp.einsum('tkgd,skd->kgts', block_of_queries, key_heads, precision=HIGHEST)
        scores = low_back(raw_scores) * HEAD_SIZE ** (-0.5)
        query_seg = lax.dynamic_slice_in_dim(seg_row, anchor_position, block_length, 0)
        allowed = (places[None, :] <= row_ids[:, None]) & (seg_row[None, :] == query_seg[:, None])
        scores = jnp.where(allowed[None, None], scores, -1e+30)
        probabilities = low(jax.nn.softmax(scores, axis=-1))
        blended = jnp.einsum('kgts,skd->tkgd', probabilities, value_heads, precision=HIGHEST)
        return blended.reshape(block_length, QUERY_HEADS_TOTAL * HEAD_SIZE)
    outputs = lax.map(jax.checkpoint(one_block), jnp.arange(sequence_length // block_length, dtype=jnp.int32))
    return outputs.reshape(sequence_length, QUERY_HEADS_TOTAL * HEAD_SIZE)

def layer(params, inputs, seg_row, starts):
    input_gain, middle_gain, mixer_gain, conv_input_weight, conv_input_bias, conv_state_weight, conv_state_bias, log_rates, step_bias, skip_gain, mixer_gate, mixer_input, step_weight, state_weight, query_weight, key_value_weight, mixer_output, attention_out, gate_weight, up_weight, down_weight = params
    sequence_length = inputs.shape[0]
    normed = low(rms_norm(inputs, input_gain))
    gate_values = low_back(matmul_high(normed, mixer_gate))
    conv_source = jnp.concatenate([low(low_back(matmul_high(normed, mixer_input))), low(low_back(matmul_high(normed, state_weight)))], axis=1)
    step_raw = low_back(matmul_high(normed, step_weight))
    query_rows = low(low_back(matmul_high(normed, query_weight)))
    key_value_rows = low(low_back(matmul_high(normed, key_value_weight)))
    positions = jnp.arange(sequence_length, dtype=jnp.int32)
    padded = jnp.concatenate([jnp.zeros((CONV - 1, conv_source.shape[1]), jnp.float32), conv_source], axis=0)
    conv_weight = jnp.concatenate([conv_input_weight, conv_state_weight], axis=1)
    conv_bias = jnp.concatenate([conv_input_bias, conv_state_bias], axis=0)
    convolved = low(conv_mix(padded, conv_weight, conv_bias, seg_row, positions))
    inner_width = HM * HP
    head_inputs = convolved[:, :inner_width].reshape(sequence_length, HM, HP)
    input_matrix = convolved[:, inner_width:inner_width + NS]
    output_matrix = convolved[:, inner_width + NS:]
    step_size = jax.nn.softplus(step_raw + step_bias)
    decay_log = step_size * -jnp.exp(log_rates)
    ssd_values = ssd_scan(head_inputs, input_matrix, output_matrix, step_size, decay_log, starts)
    ssd_values = ssd_values + skip_gain[None, :, None] * head_inputs
    gated = ssd_values.reshape(sequence_length, inner_width) * jax.nn.silu(gate_values)
    mixer_scale = lax.rsqrt(lax.optimization_barrier(jnp.mean(gated * gated, axis=-1, keepdims=True)) + EPSILON)
    pre_output = low(gated * mixer_gain)
    mixer_branch = mixer_scale * low_back(matmul_high(pre_output, mixer_output))
    head_pairing = key_value_rows.reshape(sequence_length, KEYVALUE_HEADS, 2, HEAD_SIZE)
    key_heads = head_pairing[:, :, 0, :]
    value_heads = head_pairing[:, :, 1, :]
    attended = low(low_back(attend(query_rows.reshape(sequence_length, QUERY_HEADS_TOTAL, HEAD_SIZE), key_heads, value_heads, seg_row)))
    branch = low_back(mixer_branch + matmul_high(attended, attention_out))
    residual = inputs + branch
    normed_mid = low(rms_norm(residual, middle_gain))
    gate_pre = low_back(matmul_high(normed_mid, gate_weight))
    up_pre = low_back(matmul_high(normed_mid, up_weight))
    hidden = low(jax.nn.silu(gate_pre) * up_pre)
    return residual + low_back(matmul_high(hidden, down_weight))

def reference(hidden_in, out_grad, seg_ids, seg_starts, input_gain, middle_gain, mixer_gain, conv_input_weight, conv_input_bias, conv_state_weight, conv_state_bias, log_rates, step_bias, skip_gain, mixer_gate, mixer_input, step_weight, state_weight, query_weight, key_value_weight, mixer_output, attention_out, gate_weight, up_weight, down_weight):
    params = tuple((array.astype(jnp.float32) for array in (input_gain, middle_gain, mixer_gain, conv_input_weight, conv_input_bias, conv_state_weight, conv_state_bias, log_rates, step_bias, skip_gain, mixer_gate, mixer_input, step_weight, state_weight, query_weight, key_value_weight, mixer_output, attention_out, gate_weight, up_weight, down_weight)))

    def per_sequence(totals, element):
        inputs, cotangent, seg_row, starts = element

        def forward(weights, values):
            return layer(weights, values, seg_row, starts)
        output, pullback = jax.vjp(forward, params, inputs.astype(jnp.float32))
        grad_params, grad_inputs = pullback(cotangent.astype(jnp.float32))
        totals = jax.tree.map(lambda summed, addend: summed + addend, totals, grad_params)
        return (totals, (output.astype(jnp.bfloat16), grad_inputs))
    initial = jax.tree.map(jnp.zeros_like, params)
    totals, (outputs, grads_in) = lax.scan(per_sequence, initial, (hidden_in, out_grad, seg_ids, seg_starts))
    return (outputs, grads_in, totals[0], totals[1], totals[2], totals[3], totals[4], totals[5], totals[6], totals[7], totals[8], totals[9], totals[10], totals[11], totals[12], totals[13], totals[14], totals[15], totals[16], totals[17], totals[18], totals[19], totals[20])
```

```python
import math

import jax
import jax.numpy as jnp
from jax import lax
from jax.experimental import pallas as pl
from jax.experimental.pallas import tpu as pltpu
from jax.sharding import PartitionSpec as P

HP = 64
NS = 256
CONV = 4
QUERY_HEADS_TOTAL = 8
KEYVALUE_HEADS = 2
HEAD_SIZE = 128
DI = 3072


EPSILON = 1e-05
HIGHEST = lax.Precision.HIGHEST


def carried_in(x, axis, join, neutral):
    place = lax.axis_index(axis)
    gathered = jax.tree.map(
        lambda a, kind: lax.all_gather(a.astype(kind), axis), x, (jnp.bfloat16, jnp.bfloat16)
    )
    state = jax.tree.map(lambda a, e: jnp.zeros_like(a) + jnp.asarray(e, a.dtype), x, neutral)

    def carried_one(hop, state):
        return join(
            state,
            jax.tree.map(
                lambda a, own: lax.dynamic_index_in_dim(a, hop, 0, False).astype(own.dtype),
                gathered,
                x,
            ),
        )

    return lax.fori_loop(0, place, carried_one, state)


def entering_2(x, axis, join, neutral):
    count = lax.axis_size(axis)
    place = lax.axis_index(axis)
    ahead = count - 1 - place
    gathered = jax.tree.map(
        lambda a, kind: lax.all_gather(a.astype(kind), axis),
        x,
        jax.tree.map(lambda a: jnp.bfloat16 if a.dtype == jnp.float32 else a.dtype, x),
    )
    state = jax.tree.map(lambda a, e: jnp.zeros_like(a) + jnp.asarray(e, a.dtype), x, neutral)

    def entering_one(hop, state):
        source = count - 1 - hop
        return join(
            state,
            jax.tree.map(
                lambda a, own: lax.dynamic_index_in_dim(a, source, 0, False).astype(own.dtype),
                gathered,
                x,
            ),
        )

    return lax.fori_loop(0, ahead, entering_one, state)


def rms_norm(values, gain):
    return values * lax.rsqrt(jnp.mean(values * values, axis=-1, keepdims=True) + EPSILON) * gain


def conv_mix(extended, conv_weight, conv_bias, seg_row, positions):
    tokens = positions.shape[0]
    sequence_length = seg_row.shape[0]
    summed = jnp.zeros((tokens, extended.shape[1]), jnp.float32) + conv_bias
    own_seg = seg_row[positions]
    for offset in range(CONV):
        source = positions - offset
        usable = (source >= 0) & (seg_row[jnp.clip(source, 0, sequence_length - 1)] == own_seg)
        shifted = extended[CONV - 1 - offset : CONV - 1 - offset + tokens]
        summed = summed + jnp.where(usable[:, None], shifted, 0.0) * conv_weight[CONV - 1 - offset]
    return jax.nn.silu(summed)


def ssd_block(carried, block_parts):
    input_part, bterm_part, cterm_part, step_part, decay_part, start_part = block_parts
    width = start_part.shape[0]
    cumulative = jnp.cumsum(decay_part, axis=0)
    run_ids = jnp.cumsum(start_part)
    ordinal = jnp.arange(width)
    joined = (ordinal[:, None] >= ordinal[None, :]) & (run_ids[:, None] == run_ids[None, :])
    spread = cumulative[:, None, :] - cumulative[None, :, :]
    factor = jnp.exp(jnp.where(joined[:, :, None], spread, 0.0)) * joined[:, :, None].astype(
        jnp.float32
    )
    inner_cb = jnp.einsum("tn,sn->ts", cterm_part, bterm_part, precision=HIGHEST)
    mixing = inner_cb[:, :, None] * factor * step_part[None, :, :]
    output = jnp.einsum("tsh,shp->thp", mixing, input_part, precision=HIGHEST)
    entry_keep = jnp.exp(cumulative) * (run_ids == 0)[:, None].astype(jnp.float32)
    output = output + entry_keep[:, :, None] * jnp.einsum(
        "tn,hpn->thp", cterm_part, carried, precision=HIGHEST
    )
    to_end = jnp.exp(cumulative[-1][None, :] - cumulative) * (run_ids == run_ids[-1])[
        :, None
    ].astype(jnp.float32)
    carry_on = jnp.exp(cumulative[-1]) * (run_ids[-1] == 0).astype(jnp.float32)
    weighted = (to_end * step_part)[:, :, None] * input_part
    update = jnp.einsum("shp,sn->hpn", weighted, bterm_part, precision=HIGHEST)
    return (carry_on[:, None, None] * carried + update, output)


def project(left, right):
    return jnp.dot(left, right, preferred_element_type=jnp.float32)


def project_back(left, right):
    return jnp.einsum("tc,dc->td", left, right, preferred_element_type=jnp.float32)


def weight_grad(left, right):
    return jnp.einsum("td,tc->dc", left, right, preferred_element_type=jnp.float32)


def silu_slope(values):
    logistic = jax.nn.sigmoid(values)
    return logistic * (1.0 + values * (1.0 - logistic))


def chain_combine(earlier, later):
    return (earlier[0] * later[0], later[0][:, None, None] * earlier[1] + later[1])


def fetch_weights(
    mixer_gate,
    mixer_input,
    step_weight,
    state_weight,
    query_weight,
    key_value_weight,
    mixer_output,
    attention_out,
    gate_weight,
    up_weight,
    down_weight,
):
    return (
        lax.all_gather(mixer_gate, "row", axis=0, tiled=True),
        lax.all_gather(mixer_input, "row", axis=0, tiled=True),
        lax.all_gather(step_weight, "row", axis=0, tiled=True),
        lax.all_gather(state_weight, "row", axis=0, tiled=True),
        lax.all_gather(query_weight, "row", axis=0, tiled=True),
        lax.all_gather(key_value_weight, "row", axis=0, tiled=True),
        lax.all_gather(mixer_output, "row", axis=1, tiled=True),
        lax.all_gather(attention_out, "row", axis=1, tiled=True),
        lax.all_gather(gate_weight, "row", axis=0, tiled=True),
        lax.all_gather(up_weight, "row", axis=0, tiled=True),
        lax.all_gather(down_weight, "row", axis=1, tiled=True),
    )


def col_sums(first, second):
    return (
        lax.psum_scatter(first, "col", scatter_dimension=1, tiled=True),
        lax.psum_scatter(second, "col", scatter_dimension=1, tiled=True),
    )


def per_device(
    hidden_in,
    out_grad,
    seg_ids,
    seg_starts,
    input_gain,
    middle_gain,
    mixer_gain,
    conv_input_weight,
    conv_input_bias,
    conv_state_weight,
    conv_state_bias,
    log_rates,
    step_bias,
    skip_gain,
    mixer_gate,
    mixer_input,
    step_weight,
    state_weight,
    query_weight,
    key_value_weight,
    mixer_output,
    attention_out,
    gate_weight,
    up_weight,
    down_weight,
):
    inputs = hidden_in[0].astype(jnp.float32)
    tokens = inputs.shape[0]
    seg_row = seg_ids[0]
    sequence_length = seg_row.shape[0]
    starts = seg_starts[0]
    row_index = lax.axis_index("row")
    col_index = lax.axis_index("col")
    row_count = lax.axis_size("row")
    positions = row_index * tokens + jnp.arange(tokens, dtype=jnp.int32)
    own_seg = lax.dynamic_slice_in_dim(seg_row, row_index * tokens, tokens, 0)
    gathered = fetch_weights(
        mixer_gate,
        mixer_input,
        step_weight,
        state_weight,
        query_weight,
        key_value_weight,
        mixer_output,
        attention_out,
        gate_weight,
        up_weight,
        down_weight,
    )
    (
        whole_zgate,
        whole_input,
        whole_step,
        whole_state,
        whole_query,
        whole_keyval,
        whole_mixout,
        whole_attout,
        whole_gate,
        whole_upper,
        whole_down,
    ) = gathered
    normed_f, input_pullback = jax.vjp(rms_norm, inputs, input_gain)
    normed = normed_f.astype(jnp.bfloat16)
    gate_values = project(normed, whole_zgate)
    conv_source = jnp.concatenate(
        [
            project(normed, whole_input).astype(jnp.bfloat16),
            project(normed, whole_state).astype(jnp.bfloat16),
        ],
        axis=1,
    )
    step_raw = project(normed, whole_step)
    query_rows = project(normed, whole_query).astype(jnp.bfloat16)
    keyval_part = project(normed, whole_keyval).astype(jnp.bfloat16)
    keyval_rows, tail_rows = (
        lax.all_gather(keyval_part, "row", axis=0, tiled=True),
        lax.all_gather(conv_source[tokens - (CONV - 1) :], "row", axis=0, tiled=True),
    )
    earlier_tail = lax.dynamic_slice_in_dim(
        tail_rows, jnp.maximum(row_index - 1, 0) * (CONV - 1), CONV - 1, 0
    )
    earlier_tail = jnp.where(row_index > 0, earlier_tail, jnp.zeros_like(earlier_tail))
    extended = jnp.concatenate([earlier_tail, conv_source], axis=0).astype(jnp.float32)
    conv_weight = jnp.concatenate([conv_input_weight, conv_state_weight], axis=1)
    conv_bias = jnp.concatenate([conv_input_bias, conv_state_bias], axis=0)

    def conv_local(ext_values, weight_values, bias_values):
        return conv_mix(ext_values, weight_values, bias_values, seg_row, positions)

    convolved_f, conv_pullback = jax.vjp(conv_local, extended, conv_weight, conv_bias)
    convolved = convolved_f.astype(jnp.bfloat16)
    inner_local = mixer_input.shape[1]
    state_full, keyval_full = (
        lax.all_gather(convolved[:, inner_local:], "col", axis=1, tiled=True),
        lax.all_gather(keyval_rows, "col", axis=1, tiled=True),
    )
    head_count = log_rates.shape[0]
    head_inputs = convolved[:, :inner_local].astype(jnp.float32).reshape(tokens, head_count, HP)
    input_matrix = state_full[:, :NS].astype(jnp.float32)
    output_matrix = state_full[:, NS:].astype(jnp.float32)

    def ssd_main(
        head_values, input_values, output_values, step_values, rate_values, bias_values, skip_values
    ):
        step_size = jax.nn.softplus(step_values + bias_values)
        decay_log = step_size * -jnp.exp(rate_values)
        block_length = math.gcd(tokens, 128)
        block_count = tokens // block_length
        block_parts = (
            head_values.reshape(block_count, block_length, head_count, HP),
            input_values.reshape(block_count, block_length, NS),
            output_values.reshape(block_count, block_length, NS),
            step_size.reshape(block_count, block_length, head_count),
            decay_log.reshape(block_count, block_length, head_count),
            starts.reshape(block_count, block_length),
        )
        initial = jnp.zeros((head_count, HP, NS), jnp.float32)
        last_state, outputs = lax.scan(ssd_block, initial, block_parts)
        ssd_zero = (
            outputs.reshape(tokens, head_count, HP) + skip_values[None, :, None] * head_values
        )
        passing = jnp.exp(jnp.sum(decay_log, axis=0)) * (jnp.sum(starts) == 0).astype(jnp.float32)
        return (ssd_zero, passing, last_state)

    def ssd_entry(output_values, step_values, rate_values, bias_values, carried):
        step_size = jax.nn.softplus(step_values + bias_values)
        decay_log = step_size * -jnp.exp(rate_values)
        entry_keep = jnp.exp(jnp.cumsum(decay_log, axis=0)) * (jnp.cumsum(starts) == 0)[
            :, None
        ].astype(jnp.float32)
        return entry_keep[:, :, None] * jnp.einsum(
            "tn,hpn->thp", output_values, carried, precision=HIGHEST
        )

    (ssd_zero, passing, last_state), ssd_pullback = jax.vjp(
        ssd_main,
        head_inputs,
        input_matrix,
        output_matrix,
        step_raw,
        log_rates,
        step_bias,
        skip_gain,
    )
    identity = (jnp.ones_like(passing), jnp.zeros_like(last_state))
    entering = carried_in((passing, last_state), "row", chain_combine, identity)[1]
    ssd_extra, entry_pullback = jax.vjp(
        ssd_entry, output_matrix, step_raw, log_rates, step_bias, entering
    )
    ssd_values = ssd_zero + ssd_extra
    flat_ssd = ssd_values.reshape(tokens, inner_local)
    gate_silu = jax.nn.silu(gate_values)
    gated = flat_ssd * gate_silu
    square_part = jnp.sum(gated * gated, axis=-1)
    pre_output = (gated * mixer_gain).astype(jnp.bfloat16)
    mixer_part = project(pre_output, whole_mixout)
    query_local = query_rows.shape[1] // HEAD_SIZE
    group_width = QUERY_HEADS_TOTAL // KEYVALUE_HEADS
    kv_head = col_index * query_local // group_width
    key_all = lax.dynamic_slice_in_dim(keyval_full, kv_head * 2 * HEAD_SIZE, HEAD_SIZE, 1)
    value_all = lax.dynamic_slice_in_dim(
        keyval_full, kv_head * 2 * HEAD_SIZE + HEAD_SIZE, HEAD_SIZE, 1
    )
    query_heads = query_rows.reshape(tokens, query_local, HEAD_SIZE)
    block_length = math.gcd(sequence_length, 512)
    scale = HEAD_SIZE ** (-0.5)
    seg_first = jnp.sum((seg_row < own_seg[0]).astype(jnp.int32))
    low_block = seg_first // block_length
    high_block = (row_index * tokens + tokens - 1) // block_length + 1

    def block_scores(number):
        anchor_position = number * block_length
        key_block = lax.dynamic_slice_in_dim(key_all, anchor_position, block_length, 0)
        value_block = lax.dynamic_slice_in_dim(value_all, anchor_position, block_length, 0)
        key_places = anchor_position + jnp.arange(block_length, dtype=jnp.int32)
        key_seg = lax.dynamic_slice_in_dim(seg_row, anchor_position, block_length, 0)
        allowed = (key_places[None, :] <= positions[:, None]) & (
            key_seg[None, :] == own_seg[:, None]
        )
        raw_scores = (
            jnp.einsum("thd,kd->htk", query_heads, key_block, preferred_element_type=jnp.float32)
            * scale
        )
        return (jnp.where(allowed[None], raw_scores, -1e30), key_block, value_block)

    def max_pass(number, carry):
        running_max, running_sum = carry
        scores, key_block, value_block = block_scores(number)
        new_max = jnp.maximum(running_max, jnp.max(scores, axis=-1))
        running_sum = running_sum * jnp.exp(running_max - new_max) + jnp.sum(
            jnp.exp(scores - new_max[:, :, None]), axis=-1
        )
        return (new_max, running_sum)

    running_max, running_sum = lax.fori_loop(
        low_block,
        high_block,
        max_pass,
        (
            jnp.full((query_local, tokens), -1e30, jnp.float32),
            jnp.zeros((query_local, tokens), jnp.float32),
        ),
    )
    log_total = running_max + jnp.log(running_sum)

    def value_pass(number, accum):
        scores, key_block, value_block = block_scores(number)
        probabilities = jnp.exp(scores - log_total[:, :, None])
        return accum + jnp.einsum(
            "htk,kd->thd",
            probabilities.astype(jnp.bfloat16),
            value_block,
            preferred_element_type=jnp.float32,
        )

    attended_f = lax.fori_loop(
        low_block, high_block, value_pass, jnp.zeros((tokens, query_local, HEAD_SIZE), jnp.float32)
    )
    attended = attended_f.astype(jnp.bfloat16).reshape(tokens, query_local * HEAD_SIZE)
    attn_part = project(attended, whole_attout)
    mixer_total, attn_total, square_total = lax.psum((mixer_part, attn_part, square_part), "col")
    mixer_scale = lax.rsqrt(square_total / DI + EPSILON)[:, None]
    residual = inputs + mixer_scale * mixer_total + attn_total
    normed_mid_f, mid_pullback = jax.vjp(rms_norm, residual, middle_gain)
    normed_mid = normed_mid_f.astype(jnp.bfloat16)
    gate_pre = project(normed_mid, whole_gate)
    up_pre = project(normed_mid, whole_upper)
    gate_silu_ffn = jax.nn.silu(gate_pre)
    hidden = (gate_silu_ffn * up_pre).astype(jnp.bfloat16)
    ffn_total = lax.psum(project(hidden, whole_down).astype(jnp.bfloat16), "col").astype(
        jnp.float32
    )
    layer_out = (residual + ffn_total).astype(jnp.bfloat16)
    gathered_back = fetch_weights(
        mixer_gate,
        mixer_input,
        step_weight,
        state_weight,
        query_weight,
        key_value_weight,
        mixer_output,
        attention_out,
        gate_weight,
        up_weight,
        down_weight,
    )
    (
        back_zgate,
        back_input,
        back_step,
        back_state,
        back_query,
        back_keyval,
        back_mixout,
        back_attout,
        back_gate,
        back_upper,
        back_down,
    ) = gathered_back
    cotangent = out_grad[0].astype(jnp.float32)
    ffn_grad = cotangent.astype(jnp.bfloat16)
    grad_down = weight_grad(hidden, ffn_grad)
    hidden_grad = project_back(ffn_grad, back_down)
    gate_grad = (hidden_grad * up_pre * silu_slope(gate_pre)).astype(jnp.bfloat16)
    up_grad = (hidden_grad * gate_silu_ffn).astype(jnp.bfloat16)
    grad_gate = weight_grad(normed_mid, gate_grad)
    grad_upper = weight_grad(normed_mid, up_grad)
    mid_part = project_back(gate_grad, back_gate) + project_back(up_grad, back_upper)
    mid_grad = lax.psum(mid_part.astype(jnp.bfloat16), "col").astype(jnp.float32)
    resid_extra, grad_middle_gain = mid_pullback(mid_grad)
    residual_grad = cotangent + resid_extra
    branch_grad = residual_grad.astype(jnp.bfloat16)
    branch_grad_f = branch_grad.astype(jnp.float32)
    grad_attout = weight_grad(attended, branch_grad)
    attn_grad = project_back(branch_grad, back_attout).astype(jnp.bfloat16)
    mixer_grad = (mixer_scale * branch_grad_f).astype(jnp.bfloat16)
    grad_mixout = weight_grad(pre_output, mixer_grad)
    pre_grad = project_back(mixer_grad, back_mixout)
    scale_grad = jnp.sum(branch_grad_f * mixer_total, axis=-1)
    square_grad = scale_grad * -0.5 * mixer_scale[:, 0] ** 3 / DI
    gated_grad = pre_grad * mixer_gain + 2.0 * gated * square_grad[:, None]
    grad_mixer_gain = jnp.sum(pre_grad * gated, axis=0)
    ssd_grad = (gated_grad * gate_silu).reshape(tokens, head_count, HP)
    zgate_grad = (gated_grad * flat_ssd * silu_slope(gate_values)).astype(jnp.bfloat16)
    output_grad_b, step_grad_b, rate_grad_b, bias_grad_b, entry_grad = entry_pullback(ssd_grad)
    later_grad = entering_2((passing, entry_grad), "row", chain_combine, identity)[1]
    passing_grad = jnp.sum(later_grad * entering, axis=(1, 2))
    head_grad, input_grad, output_grad, step_grad, rate_grad, bias_grad, skip_grad = ssd_pullback(
        (ssd_grad, passing_grad, later_grad)
    )
    output_grad = output_grad + output_grad_b
    step_grad = step_grad + step_grad_b
    rate_grad = rate_grad + rate_grad_b
    bias_grad = bias_grad + bias_grad_b
    attn_grad_heads = attn_grad.reshape(tokens, query_local, HEAD_SIZE)

    def delta_pass(number, accum):
        scores, key_block, value_block = block_scores(number)
        probabilities = jnp.exp(scores - log_total[:, :, None])
        prob_grad = jnp.einsum(
            "thd,kd->htk", attn_grad_heads, value_block, preferred_element_type=jnp.float32
        )
        return accum + jnp.sum(probabilities * prob_grad, axis=-1)

    delta = lax.fori_loop(
        low_block, high_block, delta_pass, jnp.zeros((query_local, tokens), jnp.float32)
    )

    def grad_pass(number, carry):
        query_grad, key_grad, value_grad = carry
        scores, key_block, value_block = block_scores(number)
        probabilities = jnp.exp(scores - log_total[:, :, None])
        prob_grad = jnp.einsum(
            "thd,kd->htk", attn_grad_heads, value_block, preferred_element_type=jnp.float32
        )
        score_grad = (probabilities * (prob_grad - delta[:, :, None]) * scale).astype(jnp.bfloat16)
        query_grad = query_grad + jnp.einsum(
            "htk,kd->thd", score_grad, key_block, preferred_element_type=jnp.float32
        )
        anchor_position = number * block_length
        key_part = jnp.einsum(
            "htk,thd->kd", score_grad, query_heads, preferred_element_type=jnp.float32
        )
        value_part = jnp.einsum(
            "htk,thd->kd",
            probabilities.astype(jnp.bfloat16),
            attn_grad_heads,
            preferred_element_type=jnp.float32,
        )
        key_grad = lax.dynamic_update_slice_in_dim(
            key_grad,
            lax.dynamic_slice_in_dim(key_grad, anchor_position, block_length, 0) + key_part,
            anchor_position,
            0,
        )
        value_grad = lax.dynamic_update_slice_in_dim(
            value_grad,
            lax.dynamic_slice_in_dim(value_grad, anchor_position, block_length, 0) + value_part,
            anchor_position,
            0,
        )
        return (query_grad, key_grad, value_grad)

    query_grad, key_grad, value_grad = lax.fori_loop(
        low_block,
        high_block,
        grad_pass,
        (
            jnp.zeros((tokens, query_local, HEAD_SIZE), jnp.float32),
            jnp.zeros((sequence_length, HEAD_SIZE), jnp.float32),
            jnp.zeros((sequence_length, HEAD_SIZE), jnp.float32),
        ),
    )
    state_grad = jnp.concatenate([input_grad, output_grad], axis=1)
    key_value_gradient = jnp.zeros((sequence_length, 2 * KEYVALUE_HEADS * HEAD_SIZE), jnp.float32)
    key_value_gradient = lax.dynamic_update_slice_in_dim(
        key_value_gradient,
        jnp.concatenate([key_grad, value_grad], axis=1),
        kv_head * 2 * HEAD_SIZE,
        1,
    )
    state_grad_part, keyval_grad_part = col_sums(state_grad, key_value_gradient)
    conv_grad_in = jnp.concatenate(
        [head_grad.reshape(tokens, inner_local), state_grad_part], axis=1
    )
    extended_grad, grad_conv_weight, grad_conv_bias = conv_pullback(conv_grad_in)
    tail_grad = jnp.where(row_index > 0, extended_grad[: CONV - 1], 0.0)
    tail_slots = jnp.zeros(((CONV - 1) * row_count, tail_grad.shape[1]), jnp.float32)
    tail_slots = lax.dynamic_update_slice_in_dim(
        tail_slots, tail_grad, jnp.maximum(row_index - 1, 0) * (CONV - 1), 0
    )
    keyval_local_grad, tail_from_next = (
        lax.psum_scatter(
            keyval_grad_part.astype(jnp.bfloat16), "row", scatter_dimension=0, tiled=True
        ).astype(jnp.float32),
        lax.psum_scatter(
            tail_slots.astype(jnp.bfloat16), "row", scatter_dimension=0, tiled=True
        ).astype(jnp.float32),
    )
    source_grad = extended_grad[CONV - 1 :]
    source_grad = jnp.concatenate(
        [source_grad[: tokens - (CONV - 1)], source_grad[tokens - (CONV - 1) :] + tail_from_next],
        axis=0,
    )
    input_pre_grad = source_grad[:, :inner_local].astype(jnp.bfloat16)
    state_pre_grad = source_grad[:, inner_local:].astype(jnp.bfloat16)
    keyval_pre_grad = keyval_local_grad.astype(jnp.bfloat16)
    query_pre_grad = query_grad.reshape(tokens, query_local * HEAD_SIZE).astype(jnp.bfloat16)
    step_pre_grad = step_grad.astype(jnp.bfloat16)
    normed_part = (
        project_back(zgate_grad, back_zgate)
        + project_back(input_pre_grad, back_input)
        + project_back(step_pre_grad, back_step)
        + project_back(state_pre_grad, back_state)
        + project_back(query_pre_grad, back_query)
        + project_back(keyval_pre_grad, back_keyval)
    )
    normed_grad = lax.psum(normed_part.astype(jnp.bfloat16), "col").astype(jnp.float32)
    input_extra, grad_input_gain = input_pullback(normed_grad)
    grad_in = (residual_grad + input_extra)[None]
    weight_grads = (
        lax.psum_scatter(
            weight_grad(normed, zgate_grad).astype(jnp.bfloat16),
            ("dp", "row"),
            scatter_dimension=0,
            tiled=True,
        ).astype(jnp.float32),
        lax.psum_scatter(
            weight_grad(normed, input_pre_grad).astype(jnp.bfloat16),
            ("dp", "row"),
            scatter_dimension=0,
            tiled=True,
        ).astype(jnp.float32),
        lax.psum_scatter(
            weight_grad(normed, step_pre_grad).astype(jnp.bfloat16),
            ("dp", "row"),
            scatter_dimension=0,
            tiled=True,
        ).astype(jnp.float32),
        lax.psum_scatter(
            weight_grad(normed, state_pre_grad).astype(jnp.bfloat16),
            ("dp", "row"),
            scatter_dimension=0,
            tiled=True,
        ).astype(jnp.float32),
        lax.psum_scatter(
            weight_grad(normed, query_pre_grad).astype(jnp.bfloat16),
            ("dp", "row"),
            scatter_dimension=0,
            tiled=True,
        ).astype(jnp.float32),
        lax.psum_scatter(
            weight_grad(normed, keyval_pre_grad).astype(jnp.bfloat16),
            ("dp", "row"),
            scatter_dimension=0,
            tiled=True,
        ).astype(jnp.float32),
        lax.psum_scatter(
            grad_mixout.astype(jnp.bfloat16), ("dp", "row"), scatter_dimension=1, tiled=True
        ).astype(jnp.float32),
        lax.psum_scatter(
            grad_attout.astype(jnp.bfloat16), ("dp", "row"), scatter_dimension=1, tiled=True
        ).astype(jnp.float32),
        lax.psum_scatter(
            grad_gate.astype(jnp.bfloat16), ("dp", "row"), scatter_dimension=0, tiled=True
        ).astype(jnp.float32),
        lax.psum_scatter(
            grad_upper.astype(jnp.bfloat16), ("dp", "row"), scatter_dimension=0, tiled=True
        ).astype(jnp.float32),
        lax.psum_scatter(
            grad_down.astype(jnp.bfloat16), ("dp", "row"), scatter_dimension=1, tiled=True
        ).astype(jnp.float32),
    )
    small_grads = lax.psum(
        (
            grad_input_gain,
            grad_middle_gain,
            grad_mixer_gain,
            grad_conv_weight[:, :inner_local],
            grad_conv_bias[:inner_local],
            grad_conv_weight[:, inner_local:],
            grad_conv_bias[inner_local:],
            rate_grad,
            bias_grad,
            skip_grad,
        ),
        ("dp", "row"),
    )
    return (
        layer_out[None],
        grad_in,
        small_grads[0],
        small_grads[1],
        small_grads[2],
        small_grads[3],
        small_grads[4],
        small_grads[5],
        small_grads[6],
        small_grads[7],
        small_grads[8],
        small_grads[9],
        weight_grads[0],
        weight_grads[1],
        weight_grads[2],
        weight_grads[3],
        weight_grads[4],
        weight_grads[5],
        weight_grads[6],
        weight_grads[7],
        weight_grads[8],
        weight_grads[9],
        weight_grads[10],
    )

HEADS_PACK = 128
BLOCK = 128


def chunk_offset(natural, place, chunk):
    mixed = ((natural & 1) << 2) | ((natural >> 2) << 1) | ((natural >> 1) & 1)
    return pl.multiple_of((mixed ^ place) * chunk, chunk)


def split_dot(left, right, dims):
    first = right.astype(jnp.bfloat16)
    rest = right - first.astype(jnp.float32)
    second = rest.astype(jnp.bfloat16)
    third = (rest - second.astype(jnp.float32)).astype(jnp.bfloat16)
    return sum(
        lax.dot_general(left, part, (dims, ((), ())), preferred_element_type=jnp.float32)
        for part in (third, second, first)
    )


def split_dot_left(left, right):
    first = left.astype(jnp.bfloat16)
    rest = left - first.astype(jnp.float32)
    second = rest.astype(jnp.bfloat16)
    third = (rest - second.astype(jnp.float32)).astype(jnp.bfloat16)
    return sum(
        lax.dot_general(part, right, (((1,), (0,)), ((), ())), preferred_element_type=jnp.float32)
        for part in (third, second, first)
    )


def mat(left, right):
    return lax.dot_general(left, right, (((1,), (0,)), ((), ())), preferred_element_type=jnp.float32)


def mat_nt(left, right):
    return lax.dot_general(left, right, (((1,), (1,)), ((), ())), preferred_element_type=jnp.float32)


def mat_tn(left, right):
    return lax.dot_general(left, right, (((0,), (0,)), ((), ())), preferred_element_type=jnp.float32)


def logistic(values):
    return 1.0 / (1.0 + jnp.exp(-values))


def block_allowed(segc_ref, segr_ref, number, width):
    rows = pl.ds(number * BLOCK, BLOCK)
    shape = (BLOCK, width)
    query_place = lax.broadcasted_iota(jnp.int32, shape, 0) + number * BLOCK
    key_place = lax.broadcasted_iota(jnp.int32, shape, 1)
    return (query_place >= key_place) & (segc_ref[rows, :] == segr_ref[:, :width])


def conv_block(padded, mask_ref, weight_ref, bias_ref, number):
    total = jnp.broadcast_to(bias_ref[0:1, :], (BLOCK, bias_ref.shape[1]))
    for offset in range(CONV):
        shifted = padded[pl.ds(8 + number * BLOCK - offset, BLOCK), :]
        usable = mask_ref[pl.ds(number * BLOCK, BLOCK), offset : offset + 1]
        total = total + (usable * shifted) * weight_ref[CONV - 1 - offset : CONV - offset, :]
    return total


def fill_padded(padded, source_ref, place, columns=None):
    chunk = source_ref.shape[0] // 8
    width = padded.shape[1]
    padded[0:8, :] = jnp.zeros((8, width), jnp.float32)
    for natural in range(8):
        rows = pl.ds(chunk_offset(natural, place, chunk), chunk)
        part = source_ref[rows, :] if columns is None else source_ref[rows, columns]
        padded[8 + chunk * natural : 8 + chunk * (natural + 1), :] = (
            part.astype(jnp.bfloat16).astype(jnp.float32)
        )


def load_block(source_ref, place, number, columns=None):
    chunk = source_ref.shape[0] // 8
    each = BLOCK // chunk
    parts = []
    for natural in range(number * each, (number + 1) * each):
        rows = pl.ds(chunk_offset(natural, place, chunk), chunk)
        parts.append(source_ref[rows, :] if columns is None else source_ref[rows, columns])
    return jnp.concatenate(parts, axis=0)


def store_block(target_ref, place, number, values):
    chunk = target_ref.shape[0] // 8
    each = BLOCK // chunk
    for part in range(each):
        rows = pl.ds(chunk_offset(number * each + part, place, chunk), chunk)
        target_ref[rows, :] = values[part * chunk : (part + 1) * chunk].astype(target_ref.dtype)


def state_conv_kernel(place_ref, raw_ref, mask_ref, weight_ref, bias_ref, out_ref, padded):
    place = place_ref[3]
    fill_padded(padded, raw_ref, place, slice(0, 128))
    blocks = out_ref.shape[0] // BLOCK

    @pl.when(place_ref[0] == 0)
    def _():
        for number in range(blocks):
            total = conv_block(padded, mask_ref, weight_ref, bias_ref, number)
            out_ref[pl.ds(number * BLOCK, BLOCK), :] = (total * logistic(total)).astype(jnp.bfloat16)

    @pl.when(place_ref[0] == 1)
    def _():
        for number in range(blocks):
            out_ref[pl.ds(number * BLOCK, BLOCK), :] = padded[
                pl.ds(8 + number * BLOCK, BLOCK), :
            ].astype(jnp.bfloat16)


def state_conv_back_kernel(
    place_ref,
    raw_ref,
    mask_ref,
    weight_ref,
    bias_ref,
    keep_ref,
    y_ref,
    d_ref,
    kv_ref,
    x_ref,
    out_ref,
    small_ref,
    padded,
    grads,
):
    place = place_ref[3]
    tokens = out_ref.shape[0]
    blocks = tokens // BLOCK
    small_ref[...] = jnp.zeros_like(small_ref)

    @pl.when(place_ref[0] == 0)
    def _():
        fill_padded(padded, raw_ref, place, slice(0, 128))
        grads[tokens : tokens + 8, :] = jnp.zeros((8, 128), jnp.float32)
        for number in range(blocks):
            rows = pl.ds(number * BLOCK, BLOCK)
            total = conv_block(padded, mask_ref, weight_ref, bias_ref, number)
            incoming = (
                keep_ref[rows, 0:128].astype(jnp.float32)
                + y_ref[rows, :].astype(jnp.float32)
                + d_ref[rows, :].astype(jnp.float32)
                + x_ref[rows, :].astype(jnp.float32)
            )
            sig = logistic(total)
            grads[rows, :] = incoming * (sig * (1.0 + total * (1.0 - sig)))
        conv_back(padded, grads, mask_ref, weight_ref, small_ref, out_ref, place, blocks)

    @pl.when(place_ref[0] == 1)
    def _():
        for number in range(blocks):
            rows = pl.ds(number * BLOCK, BLOCK)
            store_block(
                out_ref,
                place,
                number,
                kv_ref[rows, :].astype(jnp.float32) + x_ref[rows, :].astype(jnp.float32),
            )


def conv_back(padded, grads, mask_ref, weight_ref, small_ref, out_ref, place, blocks):
    for number in range(blocks):
        rows = pl.ds(number * BLOCK, BLOCK)
        own = grads[rows, :]
        small_ref[CONV : CONV + 1, :] += jnp.sum(own, axis=0, keepdims=True)
        source = jnp.zeros_like(own)
        for offset in range(CONV):
            usable = mask_ref[rows, offset : offset + 1]
            shifted = padded[pl.ds(8 + number * BLOCK - offset, BLOCK), :]
            small_ref[CONV - 1 - offset : CONV - offset, :] += jnp.sum(
                (usable * shifted) * own, axis=0, keepdims=True
            )
            later = pl.ds(number * BLOCK + offset, BLOCK)
            source = source + (
                mask_ref[later, offset : offset + 1] * grads[later, :]
            ) * weight_ref[CONV - 1 - offset : CONV - offset, :]
        store_block(out_ref, place, number, source)


def attend_kernel(
    place_ref, proj_ref, own_ref, core_ref, segc_ref, segr_ref, out_ref, lse_ref, keys, values
):
    place = place_ref[3]
    blocks = out_ref.shape[0] // BLOCK
    scale = HEAD_SIZE ** (-0.5)

    @pl.when(place_ref[2] == 0)
    def _():
        keys[...] = own_ref[...]
        values[...] = core_ref[...]

    @pl.when(place_ref[2] == 1)
    def _():
        keys[...] = core_ref[...]
        values[...] = own_ref[...]

    for number in range(blocks):
        width = (number + 1) * BLOCK
        queries = load_block(proj_ref, place, number, slice(128, 256)).astype(jnp.bfloat16)
        allowed = block_allowed(segc_ref, segr_ref, number, width)
        scores = jnp.where(allowed, mat_nt(queries, keys[0:width, :]) * scale, -1e30)
        top = jnp.max(scores, axis=1, keepdims=True)
        weights = jnp.exp(scores - top)
        total = jnp.sum(weights, axis=1, keepdims=True)
        log_total = top + jnp.log(total)
        lse_ref[pl.ds(number * BLOCK, BLOCK), :] = jnp.broadcast_to(log_total, (BLOCK, 128))
        probs = (weights / total).astype(jnp.bfloat16)
        store_block(out_ref, place, number, mat(probs, values[0:width, :]))


def attend_back_kernel(
    place_ref,
    proj_ref,
    own_ref,
    core_ref,
    segc_ref,
    segr_ref,
    lse_ref,
    grad_ref,
    out_ref,
    keep_ref,
    send_ref,
    keys,
    values,
    key_grad,
    value_grad,
):
    place = place_ref[3]
    blocks = out_ref.shape[0] // BLOCK
    scale = HEAD_SIZE ** (-0.5)

    @pl.when(place_ref[2] == 0)
    def _():
        keys[...] = own_ref[...]
        values[...] = core_ref[...]

    @pl.when(place_ref[2] == 1)
    def _():
        keys[...] = core_ref[...]
        values[...] = own_ref[...]

    key_grad[...] = jnp.zeros_like(key_grad)
    value_grad[...] = jnp.zeros_like(value_grad)
    for number in range(blocks):
        width = (number + 1) * BLOCK
        queries = load_block(proj_ref, place, number, slice(128, 256)).astype(jnp.bfloat16)
        incoming = load_block(grad_ref, place, number).astype(jnp.bfloat16)
        allowed = block_allowed(segc_ref, segr_ref, number, width)
        scores = jnp.where(allowed, mat_nt(queries, keys[0:width, :]) * scale, -1e30)
        probs = jnp.exp(scores - lse_ref[pl.ds(number * BLOCK, BLOCK), 0:1])
        prob_grad = mat_nt(incoming, values[0:width, :])
        delta = jnp.sum(probs * prob_grad, axis=1, keepdims=True)
        raw_grad = (probs * (prob_grad - delta) * scale).astype(jnp.bfloat16)
        store_block(out_ref, place, number, mat(raw_grad, keys[0:width, :]))
        key_grad[0:width, :] += mat_tn(raw_grad, queries)
        value_grad[0:width, :] += mat_tn(probs.astype(jnp.bfloat16), incoming)

    @pl.when(place_ref[2] == 0)
    def _():
        keep_ref[...] = key_grad[...].astype(jnp.bfloat16)
        send_ref[...] = value_grad[...].astype(jnp.bfloat16)

    @pl.when(place_ref[2] == 1)
    def _():
        keep_ref[...] = value_grad[...].astype(jnp.bfloat16)
        send_ref[...] = key_grad[...].astype(jnp.bfloat16)


def fill_states(place_ref, state_refs, bmat, cmat):
    own_ref, other_ref, own_core_ref, other_core_ref = state_refs

    @pl.when(place_ref[1] == 0)
    def _():
        bmat[:, 0:128] = own_ref[...]
        bmat[:, 128:256] = own_core_ref[...]
        cmat[:, 0:128] = other_ref[...]
        cmat[:, 128:256] = other_core_ref[...]

    @pl.when(place_ref[1] == 1)
    def _():
        cmat[:, 0:128] = own_ref[...]
        cmat[:, 128:256] = own_core_ref[...]
        bmat[:, 0:128] = other_ref[...]
        bmat[:, 128:256] = other_core_ref[...]


def ssd_prepare(
    place, raw_ref, proj_ref, mask_ref, weight_ref, bias_ref, head_ref, padded, pre, heads, scaled, steps, cumul, cumul_t
):
    tokens = raw_ref.shape[0]
    blocks = tokens // BLOCK
    head_count = heads.shape[1] // HP
    fill_padded(padded, raw_ref, place)
    for number in range(blocks):
        rows = pl.ds(number * BLOCK, BLOCK)
        raw_steps = load_block(proj_ref, place, number, slice(256, 384)) + head_ref[1:2, :]
        step_size = jnp.maximum(raw_steps, 0.0) + jnp.log1p(jnp.exp(-jnp.abs(raw_steps)))
        steps[rows, :] = step_size
        total = conv_block(padded, mask_ref, weight_ref, bias_ref, number)
        if pre is not None:
            pre[rows, :] = total
        rounded = (total * logistic(total)).astype(jnp.bfloat16)
        heads[rows, :] = rounded
        for head in range(head_count):
            lanes = slice(head * HP, (head + 1) * HP)
            scaled[rows, lanes] = (
                step_size[:, head : head + 1] * rounded[:, lanes].astype(jnp.float32)
            ).astype(jnp.bfloat16)
    lower = (
        lax.broadcasted_iota(jnp.int32, (tokens, tokens), 0)
        >= lax.broadcasted_iota(jnp.int32, (tokens, tokens), 1)
    ).astype(jnp.float32).astype(jnp.bfloat16)
    sums = split_dot(lower, steps[...] * head_ref[0:1, :], ((1,), (0,)))
    cumul[...] = sums
    cumul_t[...] = jnp.transpose(sums)


def ssd_kernel(
    place_ref,
    raw_ref,
    proj_ref,
    gate_ref,
    s0_ref,
    s1_ref,
    s2_ref,
    s3_ref,
    mask_ref,
    segc_ref,
    segr_ref,
    weight_ref,
    bias_ref,
    head_ref,
    wide_ref,
    out_ref,
    scan_ref,
    square_ref,
    padded,
    heads,
    scaled,
    steps,
    cumul,
    cumul_t,
    bmat,
    cmat,
):
    place = place_ref[3]
    tokens = raw_ref.shape[0]
    head_count = heads.shape[1] // HP
    fill_states(place_ref, (s0_ref, s1_ref, s2_ref, s3_ref), bmat, cmat)
    ssd_prepare(
        place, raw_ref, proj_ref, mask_ref, weight_ref, bias_ref, head_ref,
        padded, None, heads, scaled, steps, cumul, cumul_t,
    )
    for number in range(tokens // BLOCK):
        rows = pl.ds(number * BLOCK, BLOCK)
        width = (number + 1) * BLOCK
        allowed = block_allowed(segc_ref, segr_ref, number, width)
        inner = mat_nt(cmat[rows, :], bmat[0:width, :])
        for head in range(head_count):
            lanes = slice(head * HP, (head + 1) * HP)
            spread = cumul[rows, head : head + 1] - cumul_t[head : head + 1, 0:width]
            mixing = inner * jnp.exp(jnp.where(allowed, spread, -1e30))
            scan_ref[rows, lanes] = mat(mixing.astype(jnp.bfloat16), scaled[0:width, lanes])
        values = scan_ref[rows, :] + wide_ref[0:1, :] * heads[rows, :].astype(jnp.float32)
        gate = load_block(gate_ref, place, number)
        gated = values * (gate * logistic(gate))
        store_block(out_ref, place, number, gated * wide_ref[1:2, :])
        squares = jnp.sum(gated * gated, axis=1, keepdims=True)
        store_block(square_ref, place, number, jnp.broadcast_to(squares, (BLOCK, 128)))


def ssd_back_kernel(
    place_ref,
    raw_ref,
    proj_ref,
    gate_ref,
    s0_ref,
    s1_ref,
    s2_ref,
    s3_ref,
    mask_ref,
    segc_ref,
    segr_ref,
    weight_ref,
    bias_ref,
    head_ref,
    wide_ref,
    scan_ref,
    pre_grad_ref,
    pair_ref,
    gate_out_ref,
    raw_out_ref,
    step_out_ref,
    keep_ref,
    send_ref,
    small_ref,
    head_small_ref,
    padded,
    pre,
    heads,
    scaled,
    steps,
    cumul,
    cumul_t,
    bmat,
    cmat,
    grads,
    grads_low,
    back,
    b_grad,
    c_grad,
):
    place = place_ref[3]
    tokens = raw_ref.shape[0]
    blocks = tokens // BLOCK
    channels = heads.shape[1]
    head_count = channels // HP
    fill_states(place_ref, (s0_ref, s1_ref, s2_ref, s3_ref), bmat, cmat)
    ssd_prepare(
        place, raw_ref, proj_ref, mask_ref, weight_ref, bias_ref, head_ref,
        padded, pre, heads, scaled, steps, cumul, cumul_t,
    )
    small_ref[...] = jnp.zeros_like(small_ref)
    head_small_ref[...] = jnp.zeros_like(head_small_ref)
    back[...] = jnp.zeros_like(back)
    b_grad[...] = jnp.zeros_like(b_grad)
    for number in range(blocks):
        rows = pl.ds(number * BLOCK, BLOCK)
        width = (number + 1) * BLOCK
        head_block = heads[rows, :].astype(jnp.float32)
        values = scan_ref[rows, :] + wide_ref[0:1, :] * head_block
        gate = load_block(gate_ref, place, number)
        sig = logistic(gate)
        gate_silu = gate * sig
        gated = values * gate_silu
        pre_grad = load_block(pre_grad_ref, place, number)
        square_grad = load_block(pair_ref, place, number, slice(1, 2))
        gated_grad = pre_grad * wide_ref[1:2, :] + 2.0 * gated * square_grad
        small_ref[CONV + 1 : CONV + 2, :] += jnp.sum(pre_grad * gated, axis=0, keepdims=True)
        ssd_grad = gated_grad * gate_silu
        store_block(
            gate_out_ref, place, number, gated_grad * values * (sig * (1.0 + gate * (1.0 - sig)))
        )
        small_ref[CONV + 2 : CONV + 3, :] += jnp.sum(ssd_grad * head_block, axis=0, keepdims=True)
        grads[rows, :] = ssd_grad
        grads_low[rows, :] = ssd_grad.astype(jnp.bfloat16)
        allowed = block_allowed(segc_ref, segr_ref, number, width)
        inner = mat_nt(cmat[rows, :], bmat[0:width, :])
        inner_grad = jnp.zeros((BLOCK, width), jnp.float32)
        for head in range(head_count):
            lanes = slice(head * HP, (head + 1) * HP)
            spread = cumul[rows, head : head + 1] - cumul_t[head : head + 1, 0:width]
            factor = jnp.exp(jnp.where(allowed, spread, -1e30))
            own = grads_low[rows, lanes]
            inner_grad = inner_grad + mat_nt(own, scaled[0:width, lanes]) * factor
            back[0:width, lanes] += mat_tn((inner * factor).astype(jnp.bfloat16), own)
        inner_low = inner_grad.astype(jnp.bfloat16)
        c_grad[rows, :] = mat(inner_low, bmat[0:width, :])
        b_grad[0:width, :] += mat_tn(inner_low, cmat[rows, :])
    pick = (
        lax.broadcasted_iota(jnp.int32, (channels, HEADS_PACK), 0) // HP
        == lax.broadcasted_iota(jnp.int32, (channels, HEADS_PACK), 1)
    ).astype(jnp.float32).astype(jnp.bfloat16)
    upper = (
        lax.broadcasted_iota(jnp.int32, (tokens, tokens), 0)
        <= lax.broadcasted_iota(jnp.int32, (tokens, tokens), 1)
    ).astype(jnp.float32).astype(jnp.bfloat16)
    cumul_grad = split_dot_left(
        grads_low[...].astype(jnp.float32) * scan_ref[...]
        - scaled[...].astype(jnp.float32) * back[...],
        pick,
    )
    decay_grad = split_dot(upper, cumul_grad, ((1,), (0,)))
    direct = split_dot_left(heads[...].astype(jnp.float32) * back[...], pick)
    step_grad = direct + decay_grad * head_ref[0:1, :]
    head_small_ref[0:1, :] = jnp.sum(
        decay_grad * (steps[...] * head_ref[0:1, :]), axis=0, keepdims=True
    )
    grads[tokens : tokens + 8, :] = jnp.zeros((8, channels), jnp.float32)
    for number in range(blocks):
        rows = pl.ds(number * BLOCK, BLOCK)
        raw_steps = load_block(proj_ref, place, number, slice(256, 384)) + head_ref[1:2, :]
        raw_grad = step_grad[number * BLOCK : (number + 1) * BLOCK, :] * logistic(raw_steps)
        head_small_ref[1:2, :] += jnp.sum(raw_grad, axis=0, keepdims=True)
        store_block(step_out_ref, place, number, raw_grad)
        total = pre[rows, :]
        sig = logistic(total)
        slope = sig * (1.0 + total * (1.0 - sig))
        for head in range(head_count):
            lanes = slice(head * HP, (head + 1) * HP)
            head_grad = (
                steps[rows, head : head + 1] * back[rows, lanes]
                + wide_ref[0:1, lanes] * grads[rows, lanes]
            )
            grads[rows, lanes] = head_grad * slope[:, lanes]
    conv_back(padded, grads, mask_ref, weight_ref, small_ref, raw_out_ref, place, blocks)

    @pl.when(place_ref[1] == 0)
    def _():
        keep_ref[:, 0:128] = b_grad[:, 0:128].astype(jnp.bfloat16)
        keep_ref[:, 128:256] = c_grad[:, 0:128].astype(jnp.bfloat16)
        send_ref[:, 0:128] = b_grad[:, 128:256].astype(jnp.bfloat16)
        send_ref[:, 128:256] = c_grad[:, 128:256].astype(jnp.bfloat16)

    @pl.when(place_ref[1] == 1)
    def _():
        keep_ref[:, 0:128] = c_grad[:, 0:128].astype(jnp.bfloat16)
        keep_ref[:, 128:256] = b_grad[:, 0:128].astype(jnp.bfloat16)
        send_ref[:, 0:128] = c_grad[:, 128:256].astype(jnp.bfloat16)
        send_ref[:, 128:256] = b_grad[:, 128:256].astype(jnp.bfloat16)


def call_kernel(kernel, name, outs, scratch, flops, operands):
    moved = sum(math.prod(a.shape) * a.dtype.itemsize for a in operands)
    moved += sum(math.prod(s) * jnp.dtype(d).itemsize for s, d in outs)
    vmem = pl.BlockSpec(memory_space=pltpu.VMEM)
    smem = pl.BlockSpec(memory_space=pltpu.SMEM)
    return pl.pallas_call(
        kernel,
        name=name,
        out_shape=tuple(jax.ShapeDtypeStruct(s, d) for s, d in outs),
        in_specs=[smem] + [vmem] * (len(operands) - 1),
        out_specs=tuple(vmem for _ in outs),
        scratch_shapes=[pltpu.VMEM(s, d) for s, d in scratch],
        compiler_params=pltpu.CompilerParams(vmem_limit_bytes=40 * 1024 * 1024),
        cost_estimate=pl.CostEstimate(flops=flops, bytes_accessed=moved, transcendentals=flops // 500),
    )(*operands)


def swap_row(values):
    return lax.ppermute(values, "row", ((0, 1), (1, 0)))


def swap_core(values):
    return lax.ppermute(values, "col", ((0, 1), (1, 0), (2, 3), (3, 2)))


def swap_col(values):
    return lax.ppermute(values, "col", ((0, 2), (2, 0), (1, 3), (3, 1)))


def swap_both(values):
    pairs = tuple((r * 4 + c, (1 - r) * 4 + (c ^ 2)) for r in range(2) for c in range(4))
    return lax.ppermute(values, ("row", "col"), pairs)


def gather_eight(chunk):
    same_core = (chunk, swap_col(chunk), swap_row(chunk), swap_both(chunk))
    other_core = tuple(swap_core(part) for part in same_core)
    return jnp.concatenate(same_core + other_core, axis=0)


def sum_eight(partial):
    half = partial.shape[0] // 2
    chunk = half // 4
    arrived = swap_core(partial[half:])
    both = partial[:half].astype(jnp.float32) + arrived.astype(jnp.float32)
    sent = both[chunk:].astype(partial.dtype)
    return (
        both[:chunk]
        + swap_col(sent[:chunk]).astype(jnp.float32)
        + swap_row(sent[chunk : 2 * chunk]).astype(jnp.float32)
        + swap_both(sent[2 * chunk :]).astype(jnp.float32)
    )


def grouped_device(
    hidden_in,
    out_grad,
    seg_ids,
    seg_starts,
    input_gain,
    middle_gain,
    mixer_gain,
    conv_input_weight,
    conv_input_bias,
    conv_state_weight,
    conv_state_bias,
    log_rates,
    step_bias,
    skip_gain,
    mixer_gate,
    mixer_input,
    step_weight,
    state_weight,
    query_weight,
    key_value_weight,
    mixer_output,
    attention_out,
    gate_weight,
    up_weight,
    down_weight,
):
    f32, bf16 = jnp.float32, jnp.bfloat16
    row = lax.axis_index("row")
    col = lax.axis_index("col")
    yes, core = col // 2, col % 2
    first_row = row == 0
    place = jnp.stack([row, yes, core, core * 4 + row * 2 + yes]).astype(jnp.int32)
    seg_row = seg_ids[0]
    tokens = seg_row.shape[0]
    chunk = tokens // 8
    width = hidden_in.shape[2]
    half_width = width // 2

    def mine(values, axis):
        size = values.shape[axis] // 2
        return lax.dynamic_slice_in_dim(values, row * size, size, axis)

    def other(values, axis):
        size = values.shape[axis] // 2
        return lax.dynamic_slice_in_dim(values, (1 - row) * size, size, axis)

    def ordered(own, far, axis):
        return jnp.where(
            first_row, jnp.concatenate([own, far], axis), jnp.concatenate([far, own], axis)
        )

    def after(values, earlier):
        return lax.optimization_barrier((values, earlier))[0]

    own_hidden = lax.dynamic_slice_in_dim(hidden_in[0], col * chunk, chunk, 0).astype(f32)
    own_grad = lax.dynamic_slice_in_dim(out_grad[0], col * chunk, chunk, 0)
    first_scale = lax.rsqrt(jnp.mean(own_hidden * own_hidden, axis=-1, keepdims=True) + EPSILON)
    first_unit = own_hidden * first_scale
    normed = gather_eight((first_unit * input_gain).astype(bf16))

    pad = HEADS_PACK - step_weight.shape[1] // 2
    small_keep = jnp.concatenate(
        [
            jnp.where(first_row, state_weight, key_value_weight),
            mine(query_weight, 1),
            jnp.pad(mine(step_weight, 1), ((0, 0), (0, pad))),
        ],
        axis=1,
    )
    small_send = jnp.concatenate(
        [
            jnp.where(first_row, key_value_weight, state_weight),
            other(query_weight, 1),
            jnp.pad(other(step_weight, 1), ((0, 0), (0, pad))),
        ],
        axis=1,
    )
    small_far = swap_row(small_send)
    input_keep, input_far = mine(mixer_input, 1), swap_row(after(other(mixer_input, 1), small_far))
    gate_keep, gate_far = mine(mixer_gate, 1), swap_row(after(other(mixer_gate, 1), input_far))
    out_keep, out_far = mine(mixer_output, 0), swap_row(after(other(mixer_output, 0), gate_far))
    att_keep, att_far = mine(attention_out, 0), swap_row(after(other(attention_out, 0), gate_far))
    fgate_keep, fgate_far = mine(gate_weight, 1), swap_row(after(other(gate_weight, 1), out_far))
    fup_keep, fup_far = mine(up_weight, 1), swap_row(after(other(up_weight, 1), fgate_far))
    down_keep, down_far = mine(down_weight, 0), swap_row(after(other(down_weight, 0), fup_far))
    final_grad = gather_eight(after(own_grad, out_far))

    places = jnp.arange(tokens, dtype=jnp.int32)
    masks = jnp.stack(
        [
            (places >= offset) & (jnp.roll(seg_row, offset) == seg_row)
            for offset in range(CONV)
        ],
        axis=1,
    ).astype(f32)
    masks = jnp.pad(masks, ((0, 8), (0, 0)))
    seg_column = seg_row.reshape(tokens, 1)
    seg_line = seg_row.reshape(1, tokens)

    normed_own, normed_far = mine(normed, 1), other(normed, 1)

    def projected(keep, far):
        return project(normed_own, keep) + project(normed_far, far)

    small_proj = projected(small_keep, small_far)
    state_bias_line = conv_state_bias[None]
    (state_own,) = call_kernel(
        state_conv_kernel,
        "state_conv",
        [((tokens, 128), bf16)],
        [((tokens + 8, 128), f32)],
        2 * tokens * 128 * 16,
        (place, small_proj, masks, conv_state_weight, state_bias_line),
    )
    piece_y, piece_x, piece_d = swap_col(state_own), swap_row(state_own), swap_both(state_own)
    kv_own = jnp.where(first_row, piece_x, state_own)
    kv_core = swap_core(kv_own)
    state_same = jnp.where(first_row, state_own, piece_x)
    state_other = jnp.where(first_row, piece_y, piece_d)
    states = (state_same, state_other, swap_core(state_same), swap_core(state_other))

    attended, log_total = call_kernel(
        attend_kernel,
        "attend",
        [((tokens, HEAD_SIZE), bf16), ((tokens, 128), f32)],
        [((tokens, HEAD_SIZE), bf16)] * 2,
        4 * tokens * tokens * HEAD_SIZE,
        (place, small_proj, kv_own, kv_core, seg_column, seg_line),
    )
    attn_part = ordered(project(attended, att_keep), project(attended, att_far), 1).astype(bf16)
    attn_total = sum_eight(attn_part)

    input_raw = projected(input_keep, input_far).astype(bf16)
    gate_values = projected(gate_keep, gate_far)
    channels = input_raw.shape[1]
    head_count = channels // HP
    head_pad = HEADS_PACK - head_count
    head_params = jnp.pad(
        jnp.stack([-jnp.exp(mine(log_rates, 0)), mine(step_bias, 0)]), ((0, 6), (0, head_pad))
    )
    wide_params = jnp.stack([jnp.repeat(mine(skip_gain, 0), HP), mine(mixer_gain, 0)])
    conv_weight = mine(conv_input_weight, 1)
    conv_bias = mine(conv_input_bias, 0)[None]
    shared = (
        place,
        input_raw,
        small_proj,
        gate_values,
        *states,
        masks,
        seg_column,
        seg_line,
        conv_weight,
        conv_bias,
        head_params,
        wide_params,
    )
    common = [
        ((tokens, channels), bf16),
        ((tokens, channels), bf16),
        ((tokens, 128), f32),
        ((tokens, 128), f32),
        ((128, tokens), f32),
        ((tokens, NS), bf16),
        ((tokens, NS), bf16),
    ]
    pre_output, scan_values, squares = call_kernel(
        ssd_kernel,
        "ssd",
        [((tokens, channels), bf16), ((tokens, channels), f32), ((tokens, 128), f32)],
        [((tokens + 8, channels), f32)] + common,
        4 * tokens * tokens * (NS + channels),
        shared,
    )
    square_total = sum_eight(squares)[:, 0:1]
    mixer_part = ordered(project(pre_output, out_keep), project(pre_output, out_far), 1).astype(bf16)
    mixer_total = sum_eight(mixer_part)
    mixer_scale = lax.rsqrt(square_total / DI + EPSILON)
    residual = own_hidden + mixer_scale * mixer_total + attn_total
    mid_scale = lax.rsqrt(jnp.mean(residual * residual, axis=-1, keepdims=True) + EPSILON)
    mid_unit = residual * mid_scale
    normed_mid = gather_eight((mid_unit * middle_gain).astype(bf16))
    mid_own, mid_far = mine(normed_mid, 1), other(normed_mid, 1)
    gate_pre = project(mid_own, fgate_keep) + project(mid_far, fgate_far)
    up_pre = project(mid_own, fup_keep) + project(mid_far, fup_far)
    gate_silu = jax.nn.silu(gate_pre)
    hidden = (gate_silu * up_pre).astype(bf16)

    hidden_grad = project_back(mine(final_grad, 1), down_keep) + project_back(
        other(final_grad, 1), down_far
    )
    ffn_gate_grad = (hidden_grad * up_pre * silu_slope(gate_pre)).astype(bf16)
    ffn_up_grad = (hidden_grad * gate_silu).astype(bf16)
    mid_part = ordered(
        project_back(ffn_gate_grad, fgate_keep) + project_back(ffn_up_grad, fup_keep),
        project_back(ffn_gate_grad, fgate_far) + project_back(ffn_up_grad, fup_far),
        1,
    ).astype(bf16)
    mid_grad = sum_eight(mid_part)

    def scattered(values, axis):
        return lax.psum_scatter(values.astype(bf16), "dp", scatter_dimension=axis, tiled=True)

    grad_down = scattered(weight_grad(hidden, final_grad), 1)
    grad_ffn = scattered(
        weight_grad(normed_mid, jnp.concatenate([ffn_gate_grad, ffn_up_grad], axis=1)), 0
    )

    ffn_part = ordered(project(hidden, down_keep), project(hidden, down_far), 1).astype(bf16)

    def column_rows(values):
        pair = swap_core(values)
        pair = jnp.where(
            core == 0, jnp.concatenate([values, pair], 0), jnp.concatenate([pair, values], 0)
        )
        far = swap_col(pair)
        return jnp.where(yes == 0, jnp.concatenate([pair, far], 0), jnp.concatenate([far, pair], 0))

    own_cotangent = own_grad.astype(f32)
    scaled_grad = mid_grad * middle_gain
    residual_grad = own_cotangent + mid_scale * (
        scaled_grad - mid_unit * jnp.mean(scaled_grad * mid_unit, axis=-1, keepdims=True)
    )
    grad_middle_gain = jnp.sum(mid_grad * mid_unit, axis=0)
    branch_own = residual_grad.astype(bf16)
    scale_grad = jnp.sum(branch_own.astype(f32) * mixer_total, axis=-1, keepdims=True)
    square_grad = scale_grad * -0.5 * mixer_scale**3 / DI
    lane = lax.broadcasted_iota(jnp.int32, (chunk, 128), 1)
    pair_own = jnp.where(lane == 0, mixer_scale, jnp.where(lane == 1, square_grad, 0.0))
    branch_grad = gather_eight(branch_own)
    pair = gather_eight(pair_own)
    mixer_grad = (pair[:, 0:1] * branch_grad.astype(f32)).astype(bf16)
    attn_grad = (
        project_back(mine(branch_grad, 1), att_keep) + project_back(other(branch_grad, 1), att_far)
    ).astype(bf16)
    pre_grad = project_back(mine(mixer_grad, 1), out_keep) + project_back(
        other(mixer_grad, 1), out_far
    )
    query_grad, kv_keep, kv_send = call_kernel(
        attend_back_kernel,
        "attend_back",
        [((tokens, HEAD_SIZE), bf16)] * 3,
        [((tokens, HEAD_SIZE), bf16)] * 2 + [((tokens, HEAD_SIZE), f32)] * 2,
        10 * tokens * tokens * HEAD_SIZE,
        (place, small_proj, kv_own, kv_core, seg_column, seg_line, log_total, attn_grad),
    )
    kv_sum = (kv_keep.astype(f32) + swap_core(kv_send).astype(f32)).astype(bf16)
    grad_mixed = scattered(
        jnp.concatenate(
            [weight_grad(pre_output, mixer_grad), weight_grad(attended, branch_grad)], axis=0
        ),
        1,
    )
    gate_grad, input_grad, step_grad, state_keep, state_send, small_grads, head_grads = call_kernel(
        ssd_back_kernel,
        "ssd_back",
        [
            ((tokens, channels), bf16),
            ((tokens, channels), bf16),
            ((tokens, 128), bf16),
            ((tokens, NS), bf16),
            ((tokens, NS), bf16),
            ((8, channels), f32),
            ((8, 128), f32),
        ],
        [((tokens + 8, channels), f32), ((tokens, channels), f32)]
        + common
        + [
            ((tokens + 8, channels), f32),
            ((tokens, channels), bf16),
            ((tokens, channels), f32),
            ((tokens, NS), f32),
            ((tokens, NS), f32),
        ],
        10 * tokens * tokens * (NS + channels),
        shared + (scan_values, pre_grad, pair),
    )
    grad_zgate = scattered(weight_grad(normed, gate_grad), 0)
    state_sum = state_keep.astype(f32) + swap_core(state_send).astype(f32)
    state_low = state_sum.astype(bf16)
    sent_x = jnp.where(first_row, kv_sum, state_low[:, :128])
    from_x = swap_row(sent_x)
    from_y = swap_col(state_low[:, 128:])
    from_d = swap_both(state_low[:, 128:])
    mix_grad, state_small = call_kernel(
        state_conv_back_kernel,
        "state_conv_back",
        [((tokens, 128), bf16), ((8, 128), f32)],
        [((tokens + 8, 128), f32)] * 2,
        2 * tokens * 128 * 40,
        (
            place,
            small_proj,
            masks,
            conv_state_weight,
            state_bias_line,
            state_sum,
            from_y,
            from_d,
            kv_sum,
            from_x,
        ),
    )
    small_grad = jnp.concatenate([mix_grad, query_grad, step_grad], axis=1)
    normed_part = ordered(
        project_back(gate_grad, gate_keep)
        + project_back(input_grad, input_keep)
        + project_back(small_grad, small_keep),
        project_back(gate_grad, gate_far)
        + project_back(input_grad, input_far)
        + project_back(small_grad, small_far),
        1,
    ).astype(bf16)
    normed_grad = sum_eight(normed_part)
    grad_rest = scattered(
        weight_grad(normed, jnp.concatenate([input_grad, small_grad], axis=1)), 0
    )
    scaled_in = normed_grad * input_gain
    grad_own = residual_grad + first_scale * (
        scaled_in - first_unit * jnp.mean(scaled_in * first_unit, axis=-1, keepdims=True)
    )
    grad_input_gain = jnp.sum(normed_grad * first_unit, axis=0)
    grad_in = column_rows(grad_own.astype(bf16)).astype(f32)[None]
    layer_out = column_rows((residual + sum_eight(ffn_part)).astype(bf16))[None]

    def exchanged(values, axis):
        return mine(values, axis), swap_row(other(values, axis))

    def paired(values, axis, join):
        own, far = exchanged(values, axis)
        return ordered(own, far, join).astype(f32)

    out_down = paired(grad_down, 1, 0)
    ffn_own, ffn_far = exchanged(grad_ffn, 0)
    hid = ffn_gate_grad.shape[1]
    out_gate = ordered(ffn_own[:, :hid], ffn_far[:, :hid], 1).astype(f32)
    out_up = ordered(ffn_own[:, hid:], ffn_far[:, hid:], 1).astype(f32)
    mixed_own, mixed_far = exchanged(grad_mixed, 1)
    out_mixout = ordered(mixed_own[:channels], mixed_far[:channels], 0).astype(f32)
    out_attout = ordered(mixed_own[channels:], mixed_far[channels:], 0).astype(f32)
    out_zgate = paired(grad_zgate, 0, 1)
    rest_own, rest_far = exchanged(grad_rest, 0)
    out_input = ordered(rest_own[:, :channels], rest_far[:, :channels], 1).astype(f32)
    start = channels
    mix_own, mix_far = rest_own[:, start : start + 128], rest_far[:, start : start + 128]
    out_state = jnp.where(first_row, mix_own, mix_far).astype(f32)
    out_keyval = jnp.where(first_row, mix_far, mix_own).astype(f32)
    start += 128
    out_query = ordered(
        rest_own[:, start : start + 128], rest_far[:, start : start + 128], 1
    ).astype(f32)
    start += 128
    out_step = ordered(
        rest_own[:, start : start + head_count], rest_far[:, start : start + head_count], 1
    ).astype(f32)

    def spread_half(values):
        empty = jnp.zeros_like(values)
        return ordered(values, empty, values.ndim - 1)

    head_line = jnp.stack(
        [
            head_grads[0, :head_count],
            head_grads[1, :head_count],
            jnp.sum(small_grads[CONV + 2].reshape(head_count, HP), axis=1),
        ]
    )
    wide_sums, head_sums, state_sums = lax.psum(
        (spread_half(small_grads[: CONV + 2]), spread_half(head_line), state_small[: CONV + 1]),
        ("dp", "row"),
    )
    gain_sums = lax.psum(jnp.stack([grad_input_gain, grad_middle_gain]), ("dp", "row", "col"))
    return (
        layer_out,
        grad_in,
        gain_sums[0],
        gain_sums[1],
        wide_sums[CONV + 1],
        wide_sums[:CONV],
        wide_sums[CONV],
        state_sums[:CONV],
        state_sums[CONV],
        head_sums[0],
        head_sums[1],
        head_sums[2],
        out_zgate,
        out_input,
        out_step,
        out_state,
        out_query,
        out_keyval,
        out_mixout,
        out_attout,
        out_gate,
        out_up,
        out_down,
    )


def solution(mesh):
    placed = (
        P("dp", "row", None),
        P("dp", "row", None),
        P("dp", None),
        P("dp", "row"),
        P(),
        P(),
        P("col"),
        P(None, "col"),
        P("col"),
        P(None, "col"),
        P("col"),
        P("col"),
        P("col"),
        P("col"),
        P("row", "col"),
        P("row", "col"),
        P("row", "col"),
        P("row", "col"),
        P("row", "col"),
        P("row", "col"),
        P("col", "row"),
        P("col", "row"),
        P("row", "col"),
        P("row", "col"),
        P("col", "row"),
    )

    def placed_device(*operands):
        tokens = operands[2].shape[1]
        if mesh.shape["row"] == 2 and mesh.shape["col"] == 4 and tokens == 512:
            return grouped_device(*operands)
        return per_device(*operands)

    return jax.shard_map(
        placed_device,
        mesh=mesh,
        in_specs=placed,
        out_specs=(
            P("dp", "row", None),
            P("dp", "row", None),
            P(),
            P(),
            P("col"),
            P(None, "col"),
            P("col"),
            P(None, "col"),
            P("col"),
            P("col"),
            P("col"),
            P("col"),
            P(("dp", "row"), "col"),
            P(("dp", "row"), "col"),
            P(("dp", "row"), "col"),
            P(("dp", "row"), "col"),
            P(("dp", "row"), "col"),
            P(("dp", "row"), "col"),
            P("col", ("dp", "row")),
            P("col", ("dp", "row")),
            P(("dp", "row"), "col"),
            P(("dp", "row"), "col"),
            P("col", ("dp", "row")),
        ),
        check_vma=False,
    )
```
